32 devices in a mesh: lat: 8 (over z, y), tok: 4 (over x, core).
Axes of the slice: x: 2, y: 2, z: 4, core: 2. Of those that a mesh axis runs over, the one named last changes fastest.
Arguments:
- coefficients: bfloat16 [256, 16, 128], P(('lat', 'tok')), may hold values from 0 to 2
- block_ids: int32 [256, 16], P(('lat', 'tok')), may hold values from 0 to 1023, all different within a row; in each aligned block of 32 rows (0 to 31, 32 to 63, ...) at most 2 rows name the same one
- counts: int32 [256], P(('lat', 'tok')), may hold values from 10 to 16
- decoder: bfloat16 [1, 131072, 5120], P(None, 'lat', 'tok'), may hold values from -0.125 to 0.125
- bias: float32 [1, 5120], P(None, 'tok'), may hold values from -3 to 3
Outputs:
- recon: bfloat16 [1, 256, 5120], P(None, 'lat', 'tok')
The draws below stay inside these ranges and needn't reach their ends.
Inputs may be any that keep to these rules, and one draw needn't show every extreme that they name: `block_ids`: the 16 slots of a token name different blocks. Among the tokens of one index of lat (aligned blocks of 32 rows), no block is named by more than 2 slots, live or padding, and some block is named by exactly 2. `counts`: slots below a token's count are live, the others padding.
All inputs are finite; a program needn't handle non-finite values.
Results may differ from the reference program's by a relative error of at most 0.001.
Values may be sent and summed in bfloat16 or wider, within the bound.
A program may use at most 128 MiB of HBM per device.

```python
import math
import jax
import jax.numpy as jnp
import numpy as np
from jax import lax

D = 5120
BLOCKS = 1024
BLOCK = 128
ACTIVE = 16
LAYERS = 1
TOK_LAT = 32
TOKENS = 256
LATENTS = 131072
MOST = 2
N_LAT = 8


def set_ends(array, stream_key, smallest, high):
    spot = [jax.random.randint(jax.random.fold_in(stream_key, axis), (), 0, length) for axis, length in enumerate(array.shape)]
    widest = array.shape.index(max(array.shape))
    next_to = spot[:widest] + [(spot[widest] + 1) % array.shape[widest]] + spot[widest + 1:]
    return array.at[tuple(spot)].set(smallest).at[tuple(next_to)].set(high)


def block_scale(key, shape, shards, least, high):
    gain = 1.0
    for dim, shards_of in shards:
        steps = jax.random.uniform(jax.random.fold_in(jax.random.fold_in(key, 6), dim), (shards_of,), jnp.float32, least / len(shards), high / len(shards))
        gain = gain * jnp.repeat(jnp.exp(steps), shape[dim] // shards_of).reshape((-1,) + (1,) * (len(shape) - 1 - dim))
    return gain


def shared_out(key, own, number, rows, number_of, top, bound, skew):
    order = jax.random.permutation(key, number_of)
    packed, ordinary = shares(number_of, rows * top, bound, skew, True), shares(number_of, rows * top, bound, skew, False)
    places = jnp.arange(number_of)

    def named(tallies, rotation):
        used = int((tallies > 0).sum())
        fixed = max(1, used // 4)
        passed = fixed + (places - fixed + rotation * (used - fixed)) % max(1, number_of - fixed)
        return jnp.zeros((number_of,), jnp.int32).at[order[jnp.where(places < fixed, places, passed)]].set(jnp.asarray(tallies, jnp.int32))

    tallies = jnp.where(number % 4 == 0, named(packed, number // 4), named(ordinary, number - number // 4 - 1))
    mixed = jax.random.permutation(jax.random.fold_in(own, 3), number_of)
    source_of, receiver = mixed[0:number_of // 2 * 2:2], mixed[1:number_of // 2 * 2:2]
    slack = jnp.minimum(tallies[source_of] - 1, bound - tallies[receiver]) // 2
    slack = jnp.where((source_of == order[0]) | (receiver == order[0]) | (tallies[receiver] == 0), 0, jnp.maximum(slack, 0))
    passed = jax.random.randint(jax.random.fold_in(own, 4), (number_of // 2,), 0, 1 << 20) % (slack + 1)
    tallies = tallies.at[source_of].add(-passed).at[receiver].add(passed)
    members = jnp.searchsorted(jnp.cumsum(tallies), jnp.arange(rows * top), side="right").astype(jnp.int32)
    grid = members.reshape(top, rows).T
    grid = grid[jax.random.permutation(jax.random.fold_in(own, 1), rows)]
    rotation = jax.random.randint(jax.random.fold_in(own, 2), (rows, 1), 0, top)
    return jnp.take_along_axis(grid, (jnp.arange(top)[None, :] + rotation) % top, axis=1)


def shares(amount, total, bound, lean, full):
    portions = [(1 << 20) // math.isqrt(standing ** lean) + 1 for standing in range(1, amount + 1)]
    largest = bound if full else min(bound, max(-(-total // amount), total * portions[0] // sum(portions)))
    least = 1 if total - largest >= amount - 1 else 0
    holding, surplus = [largest] + [least] * (amount - 1), total - largest - least * (amount - 1)
    while surplus > 0:
        free = [i for i in range(1, amount) if holding[i] < largest] or [i for i in range(1, amount) if holding[i] < bound]
        pool, remaining = sum([portions[i] for i in free]), surplus
        for i in free:
            addition = min(bound - holding[i], max(1, remaining * portions[i] // pool), surplus)
            holding[i] = holding[i] + addition
            surplus = surplus - addition
    return np.array(holding)


def scatter_about(key, extent, deviation, limit, pieces=(), held_as=jnp.bfloat16):
    result = jax.random.normal(key, extent, jnp.float32) * deviation
    if len(pieces) > 0:
        result = block_scale(key, extent, pieces, -0.22, 0.18) * result
    return jnp.clip(result, min=-limit, max=limit).astype(held_as)


def setup_inputs(seed: int = 0) -> dict:
    splits = jax.random.split(jax.random.key(seed), 6)
    coefficients = jnp.clip(2.0 * jax.random.uniform(splits[0], (TOKENS, ACTIVE, BLOCK), jnp.float32) ** block_scale(splits[0], (TOKENS, ACTIVE, BLOCK), ((0, 32),), -0.2, 0.2), 0.0, 2.0).astype(jnp.bfloat16)
    block_ids_keys = jax.random.split(jax.random.fold_in(splits[1], 1), TOKENS // TOK_LAT)
    block_ids_turns = jax.random.permutation(jax.random.fold_in(splits[1], 3), TOKENS // TOK_LAT)
    block_ids = jax.vmap(lambda own, number: shared_out(jax.random.fold_in(splits[1], 2), own, number, TOK_LAT, BLOCKS, ACTIVE, MOST, 2))(block_ids_keys, block_ids_turns).reshape((TOKENS, ACTIVE))
    counts = set_ends(jax.random.randint(splits[2], (TOKENS,), ACTIVE - ACTIVE * 3 // 8, ACTIVE + 1), jax.random.fold_in(splits[2], 1), ACTIVE - ACTIVE * 3 // 8, ACTIVE).astype(jnp.int32)
    decoder = scatter_about(splits[3], (LAYERS, LATENTS, D), (ACTIVE * BLOCK) ** -0.5, 0.125, ((1, 8), (2, 4)))
    bias = scatter_about(splits[4], (LAYERS, D), 0.5, 3.0, ((1, 4),), jnp.float32)
    return dict(coefficients=coefficients, block_ids=block_ids, counts=counts, decoder=decoder, bias=bias)


def slot_ranks(identity_row):
    length_total = identity_row.shape[0]
    serial = jnp.arange(length_total, dtype=jnp.int32)
    matches = (identity_row[:, None] == identity_row[None, :]) & (serial[None, :] < serial[:, None])
    return jnp.sum(matches.astype(jnp.int32), axis=1).astype(jnp.int32)


def reference(coefficients, block_ids, counts, decoder, bias):
    token_total = coefficients.shape[0]
    is_live = jnp.arange(ACTIVE, dtype=jnp.int32)[None, :] < counts[:, None]
    active_coeffs = jnp.where(is_live[:, :, None], coefficients, jnp.zeros((), coefficients.dtype))
    grouped = block_ids.reshape(N_LAT, TOK_LAT * ACTIVE)
    ranked = lax.map(slot_ranks, grouped)
    capacity = N_LAT * MOST
    sources = jnp.arange(N_LAT, dtype=jnp.int32)[:, None]
    position = (grouped * capacity + sources * MOST + ranked).reshape(-1).astype(jnp.int32)
    buffer = jnp.zeros((BLOCKS * capacity, BLOCK), coefficients.dtype).at[position].set(active_coeffs.reshape(-1, BLOCK))
    token_of = jnp.arange(token_total * ACTIVE, dtype=jnp.int32) // ACTIVE
    owners = jnp.zeros((BLOCKS * capacity,), jnp.int32).at[position].set(token_of)
    buffer = buffer.reshape(BLOCKS, capacity, BLOCK)
    owners = owners.reshape(BLOCKS, capacity)
    weights = decoder.reshape(LAYERS, BLOCKS, BLOCK, D)
    stride_blocks = math.gcd(BLOCKS, 16)

    def accumulate(summed, block_index):
        first_block = (block_index * stride_blocks).astype(jnp.int32)
        piece = lax.dynamic_slice_in_dim(buffer, first_block, stride_blocks, 0).astype(jnp.float32)
        weight_piece = lax.dynamic_slice_in_dim(weights, first_block, stride_blocks, 1).astype(jnp.float32)
        slot_rows = jnp.einsum("bmk,lbkd->lbmd", piece, weight_piece)
        targets = lax.dynamic_slice_in_dim(owners, first_block, stride_blocks, 0).reshape(-1)
        return summed.at[:, targets, :].add(slot_rows.reshape(LAYERS, -1, D)), None

    start_total = jnp.zeros((LAYERS, token_total, D), jnp.float32)
    summed, _ = lax.scan(accumulate, start_total, jnp.arange(BLOCKS // stride_blocks, dtype=jnp.int32))
    return (summed + bias[:, None, :]).astype(jnp.bfloat16)
```

```python
import functools

import jax
import jax.numpy as jnp
from jax import lax
from jax.experimental import pallas as pl
from jax.experimental.pallas import tpu as pltpu
from jax.sharding import PartitionSpec as P

MESH = pl.DeviceIdType.MESH
F32 = jnp.float32
BF16 = jnp.bfloat16


def largest_divisor(total, limit, unit):
    best = unit
    for size in range(unit, limit + 1, unit):
        if total % size == 0:
            best = size
    return best


def kernel(cfg, counts_ref, ids_ref, bias_ref, coeff_ref, dec_ref, out_ref,
           gath, wv, amat, part, yrecv, ysum, zrecv,
           own_sem, w_sem, zs, zr, hs, hr, cs, cr, ys, yr, ps, pr):
    nl, nt, tpd, slots, block, nb, chunks, wc, kstep, mstep, bstep = cfg
    nz, nx = nl // 2, nt // 2
    rows_dev = tpd * slots
    pack_rows = gath.shape[4]
    half = rows_dev // 2
    lat, tok = lax.axis_index("lat"), lax.axis_index("tok")
    z, y = lat // 2, lat % 2
    x, core = tok // 2, tok % 2
    oy, oc = 1 - y, 1 - core
    latents = nb * block

    w_copies = []
    for c in range(chunks):
        cols = pl.ds(c * wc, wc)
        cp = pltpu.make_async_copy(dec_ref.at[:, cols], wv.at[:, cols], w_sem.at[c])
        w_copies.append(cp)
    own = pltpu.make_async_copy(coeff_ref, gath.at[z, y, x, core, pl.ds(0, rows_dev)], own_sem)
    own.start()
    for cp in w_copies:
        cp.start()

    ids = ids_ref[...]
    trow = lax.broadcasted_iota(jnp.int32, (tpd, slots), 0)
    scol = lax.broadcasted_iota(jnp.int32, (tpd, slots), 1)
    live_to = jnp.zeros((tpd, slots), jnp.int32)
    for t in range(tpd):
        live_to = jnp.where(trow == t, counts_ref[t], live_to)
    idf = ids.astype(F32)
    owner = jnp.floor((idf + 0.5) * (1.0 / nb))
    within = idf - owner * nb
    owner = jnp.where(scol < live_to, owner, -1.0)
    srow = lax.broadcasted_iota(jnp.int32, (slots, rows_dev), 0)
    jcol = lax.broadcasted_iota(jnp.int32, (slots, rows_dev), 1)
    spread = jnp.where(jcol % slots == srow, 1.0, 0.0).astype(F32)
    t8 = lax.broadcasted_iota(jnp.int32, (tpd, rows_dev), 0)
    j8 = lax.broadcasted_iota(jnp.int32, (tpd, rows_dev), 1)
    mine = (j8 >= t8 * slots) & (j8 < (t8 + 1) * slots)

    def as_row(v):
        wide = jnp.dot(v, spread, preferred_element_type=F32)
        return jnp.sum(jnp.where(mine, wide, 0.0), axis=0, keepdims=True)

    r16 = lax.broadcasted_iota(jnp.int32, (pack_rows - rows_dev, rows_dev), 0)
    packed = jnp.where(r16 == 0, as_row(owner), jnp.where(r16 == 1, as_row(within), 0.0))
    gath[z, y, x, core, rows_dev:pack_rows, :] = packed.astype(BF16)

    zpeer = [lax.rem(z + d, nz) for d in range(1, nz)]
    xpeer = [lax.rem(x + d, nx) for d in range(1, nx)]
    peers = [(p * 2 + y, tok) for p in zpeer]
    peers += [(z * 2 + oy, tok), (lat, x * 2 + oc)]
    peers += [(lat, p * 2 + core) for p in xpeer]
    barrier = pltpu.get_barrier_semaphore()
    for p in peers:
        pl.semaphore_signal(barrier, inc=1, device_id=p, device_id_type=MESH)
    pl.semaphore_wait(barrier, len(peers))

    sent = []

    def send(src, dst, ssem, rsem, dev):
        cp = pltpu.make_async_remote_copy(src_ref=src, dst_ref=dst, send_sem=ssem,
                                          recv_sem=rsem, device_id=dev, device_id_type=MESH)
        cp.start()
        sent.append(cp)
        return cp

    def move(view, ssem, rsem, dev):
        return send(view, view, ssem, rsem, dev)

    h0, h1 = pl.ds(0, half), pl.ds(half, pack_rows - half)
    yp, cp_dev = (z * 2 + oy, tok), (lat, x * 2 + oc)
    own.wait()
    first = [move(gath.at[z, y, x, core], zs.at[d], zr.at[d], (zpeer[d] * 2 + y, tok))
             for d in range(nz - 1)]
    for cp in first:
        cp.wait_recv()
    xa = [move(gath.at[:, y, x, core, h0], hs.at[0, d], hr.at[0, d], (lat, xpeer[d] * 2 + core))
          for d in range(nx - 1)]
    ya = move(gath.at[:, y, x, core, h1], hs.at[1, 0], hr.at[1, 0], yp)
    got = [move(gath.at[:, y, x, core], cs.at[0], cr.at[0], cp_dev)]
    for cp in xa:
        cp.wait_recv()
    yb = move(gath.at[:, y, :, core, h0], hs.at[2, 0], hr.at[2, 0], yp)
    ya.wait_recv()
    xb = [move(gath.at[:, :, x, core, h1], hs.at[3, d], hr.at[3, d], (lat, xpeer[d] * 2 + core))
          for d in range(nx - 1)]
    for d in range(nx - 1):
        src = lax.rem(x + nx - 1 - d, nx)
        got.append(move(gath.at[:, y, src, core, h0], cs.at[1 + d], cr.at[1 + d], cp_dev))
    base = nx
    got.append(move(gath.at[:, oy, x, core, h1], cs.at[base], cr.at[base], cp_dev))

    lat_f = lat.astype(F32)
    pair = 2 * rows_dev
    pt = 2 * tpd
    tb = lax.broadcasted_iota(jnp.int32, (pt, pair), 0)
    jb = lax.broadcasted_iota(jnp.int32, (pt, pair), 1)
    diag = jnp.where((jb >= tb * slots) & (jb < (tb + 1) * slots), 1.0, 0.0).astype(BF16)

    def build(zz, yy, xx):
        locs = []
        for c in range(2):
            tags = gath[zz, yy, xx, c, rows_dev:pack_rows, :].astype(F32)
            locs.append(jnp.where(tags[0:1] == lat_f, tags[1:2], -1.0))
        loc = jnp.concatenate(locs, axis=1)
        loc = jnp.broadcast_to(loc, (pt, pair)).astype(BF16)
        rhs = gath[zz, yy, xx, :, 0:rows_dev, :].reshape(pair, block)
        row0 = pl.multiple_of(((zz * 2 + yy) * nx + xx) * pt, pt)
        for b0 in range(0, nb, bstep):
            hot = jnp.concatenate(
                [jnp.where(loc == jnp.asarray(b, BF16), diag, jnp.zeros((), BF16))
                 for b in range(b0, b0 + bstep)], axis=0)
            rows = jnp.dot(hot, rhs, preferred_element_type=F32).astype(BF16)
            for i in range(bstep):
                amat[pl.ds(row0, pt), (b0 + i) * block:(b0 + i + 1) * block] = (
                    rows[i * pt:(i + 1) * pt])

    got[0].wait_recv()

    @pl.loop(0, nz)
    def _(zz):
        build(zz, y, x)

    yb.wait_recv()
    got.append(move(gath.at[:, oy, :, core, h0], cs.at[base + 1], cr.at[base + 1], cp_dev))
    for d in range(nx - 1):
        xb[d].wait_recv()
        src = lax.rem(x + nx - 1 - d, nx)
        got.append(move(gath.at[:, :, src, core, h1], cs.at[base + 2 + d], cr.at[base + 2 + d], cp_dev))
    for cp in got[1:]:
        cp.wait_recv()

    @pl.loop(0, nz * (2 * nx - 1))
    def _(i):
        zz, q = i // (2 * nx - 1), i % (2 * nx - 1) + 1
        build(zz, lax.rem(y + q // nx, 2), lax.rem(x + q % nx, nx))

    tokens = amat.shape[0]
    per_lat = tokens // nl

    def matmul(c):
        cols = pl.ds(c * wc, wc)

        @pl.loop(0, tokens // mstep)
        def _(m):
            rows = pl.ds(pl.multiple_of(m * mstep, mstep), mstep)
            lats = pl.ds(m * (mstep // (2 * per_lat)), mstep // (2 * per_lat))
            shape = (mstep // (2 * per_lat), 2, per_lat, wc)

            def term(k):
                kk = pl.ds(pl.multiple_of(k * kstep, kstep), kstep)
                return jnp.dot(amat[rows, kk], wv[kk, cols],
                               preferred_element_type=F32).reshape(shape)

            part[c, lats] = term(0)

            @pl.loop(1, latents // kstep)
            def _(k):
                part[c, lats] += term(k)

    def y_start(c):
        return send(part.at[c, :, oy], yrecv.at[c], ys.at[c], yr.at[c], yp)

    def z_start(c, ycp):
        ycp.wait_recv()
        ysum[c] = part[c, :, y] + yrecv[c]
        return [send(ysum.at[c, zpeer[d]], zrecv.at[c, d], ps.at[c, d], pr.at[c, d],
                     (zpeer[d] * 2 + y, tok)) for d in range(nz - 1)]

    def finish(c, zcps):
        total = ysum[c, z] + bias_ref[:, c * wc:(c + 1) * wc]
        for d, cp in enumerate(zcps):
            cp.wait_recv()
            total += zrecv[c, d]
        out_ref[:, c * wc:(c + 1) * wc] = total.astype(out_ref.dtype)

    ycps, zcps = {}, {}
    for c in range(chunks + 2):
        if c < chunks:
            w_copies[c].wait()
            matmul(c)
            ycps[c] = y_start(c)
        if 0 <= c - 1 < chunks:
            zcps[c - 1] = z_start(c - 1, ycps[c - 1])
        if 0 <= c - 2 < chunks:
            finish(c - 2, zcps[c - 2])
    for cp in sent:
        cp.wait_send()


def shards(coefficients, block_ids, counts, decoder, bias):
    nl, nt = lax.axis_size("lat"), lax.axis_size("tok")
    tpd, slots, block = coefficients.shape
    layers, latents, width = decoder.shape
    nb = latents // block
    tokens = tpd * nl * nt
    nz, nx = nl // 2, nt // 2
    per_lat = tokens // nl
    rows_dev = tpd * slots
    pack_rows = rows_dev + 16
    wc = largest_divisor(width, 256, 128)
    chunks = width // wc
    kstep = largest_divisor(latents, 2048, block)
    mstep = largest_divisor(tokens, 256, 2 * per_lat)
    bstep = largest_divisor(nb, 32, 1)
    cfg = (nl, nt, tpd, slots, block, nb, chunks, wc, kstep, mstep, bstep)
    dma = pltpu.SemaphoreType.DMA
    vmem = pl.BlockSpec(memory_space=pltpu.VMEM)
    hbm = pl.BlockSpec(memory_space=pl.ANY)
    flops = 2 * tokens * latents * width
    outs = []
    for layer in range(layers):
        outs.append(pl.pallas_call(
            functools.partial(kernel, cfg),
            out_shape=jax.ShapeDtypeStruct((per_lat, width), BF16),
            in_specs=[pl.BlockSpec(memory_space=pltpu.SMEM), vmem, vmem, hbm, hbm],
            out_specs=vmem,
            scratch_shapes=[
                pltpu.VMEM((nz, 2, nx, 2, pack_rows, block), BF16),
                pltpu.VMEM((latents, width), BF16),
                pltpu.VMEM((tokens, latents), BF16),
                pltpu.VMEM((chunks, nz, 2, per_lat, wc), F32),
                pltpu.VMEM((chunks, nz, per_lat, wc), F32),
                pltpu.VMEM((chunks, nz, per_lat, wc), F32),
                pltpu.VMEM((chunks, nz - 1, per_lat, wc), F32),
                dma, dma((chunks,)),
                dma((nz - 1,)), dma((nz - 1,)),
                dma((4, nx - 1)), dma((4, nx - 1)),
                dma((2 * nx + 1,)), dma((2 * nx + 1,)),
                dma((chunks,)), dma((chunks,)),
                dma((chunks, nz - 1)), dma((chunks, nz - 1)),
            ],
            compiler_params=pltpu.CompilerParams(
                collective_id=layer, has_side_effects=True, vmem_limit_bytes=66000000),
            cost_estimate=pl.CostEstimate(
                flops=flops, bytes_accessed=latents * width * 2, transcendentals=0),
        )(counts, block_ids, bias[layer:layer + 1], coefficients.reshape(rows_dev, block),
          decoder[layer]))
    return jnp.stack(outs)


def solution(mesh):
    in_specs = (
        P(("lat", "tok"), None, None),
        P(("lat", "tok"), None),
        P(("lat", "tok")),
        P(None, "lat", "tok"),
        P(None, "tok"),
    )
    out_specs = P(None, "lat", "tok")
    return jax.shard_map(shards, mesh=mesh, in_specs=in_specs, out_specs=out_specs, check_vma=False)
```

```python
import functools

import jax
import jax.numpy as jnp
from jax import lax
from jax.experimental import pallas as pl
from jax.experimental.pallas import tpu as pltpu
from jax.sharding import PartitionSpec as P

MESH = pl.DeviceIdType.MESH
F32 = jnp.float32
BF16 = jnp.bfloat16


def largest_divisor(total, limit, unit):
    best = unit
    for size in range(unit, limit + 1, unit):
        if total % size == 0:
            best = size
    return best


def flip(z, k):
    step, out = 1, z
    while step <= k:
        if k & step:
            out = out + step - 2 * step * ((z // step) % 2)
        step *= 2
    return out


def kernel(cfg, counts_ref, ids_ref, bias_ref, coeff_ref, dec_ref, out_ref,
           gath, wv, amat, part, yrecv, ysum, zrecv,
           own_sem, w_sem, zs, zr, xs, xr, vs, vr, ds, dr, cs, cr, ys, yr, ps, pr):
    nl, nt, tpd, slots, block, nb, widths, rw, kstep, mstep, bstep, wsplit = cfg
    nz, nx = nl // 2, nt // 2
    rows_dev = tpd * slots
    pack_rows = gath.shape[4]
    lat, tok = lax.axis_index("lat"), lax.axis_index("tok")
    z, y = lat // 2, lat % 2
    x, core = tok // 2, tok % 2
    oy, oc = 1 - y, 1 - core
    latents = nb * block
    offs = [sum(widths[:i]) for i in range(len(widths))]

    w_copies = []
    for off, w in zip(offs, widths):
        parts = wsplit * w // widths[0]
        for r in range(parts):
            at = (pl.ds(r * (latents // parts), latents // parts), pl.ds(off, w))
            w_copies.append(pltpu.make_async_copy(dec_ref.at[at], wv.at[at],
                                                  w_sem.at[len(w_copies)]))
    w_first = [sum(wsplit * w // widths[0] for w in widths[:i]) for i in range(len(widths) + 1)]
    issued = [0]

    def stream(upto):
        while issued[0] < min(upto, len(w_copies)):
            w_copies[issued[0]].start()
            issued[0] += 1

    own = pltpu.make_async_copy(coeff_ref, gath.at[z, y, x, core, pl.ds(0, rows_dev)], own_sem)
    own.start()
    stream(2)

    ids = ids_ref[...]
    trow = lax.broadcasted_iota(jnp.int32, (tpd, slots), 0)
    scol = lax.broadcasted_iota(jnp.int32, (tpd, slots), 1)
    live_to = jnp.zeros((tpd, slots), jnp.int32)
    for t in range(tpd):
        live_to = jnp.where(trow == t, counts_ref[t], live_to)
    idf = ids.astype(F32)
    owner = jnp.floor((idf + 0.5) * (1.0 / nb))
    within = idf - owner * nb
    owner = jnp.where(scol < live_to, owner, -1.0)
    srow = lax.broadcasted_iota(jnp.int32, (slots, rows_dev), 0)
    jcol = lax.broadcasted_iota(jnp.int32, (slots, rows_dev), 1)
    spread = jnp.where(jcol % slots == srow, 1.0, 0.0).astype(F32)
    t8 = lax.broadcasted_iota(jnp.int32, (tpd, rows_dev), 0)
    j8 = lax.broadcasted_iota(jnp.int32, (tpd, rows_dev), 1)
    mine = (j8 >= t8 * slots) & (j8 < (t8 + 1) * slots)

    def as_row(v):
        wide = jnp.dot(v, spread, preferred_element_type=F32)
        return jnp.sum(jnp.where(mine, wide, 0.0), axis=0, keepdims=True)

    r16 = lax.broadcasted_iota(jnp.int32, (pack_rows - rows_dev, rows_dev), 0)
    packed = jnp.where(r16 == 0, as_row(owner), jnp.where(r16 == 1, as_row(within), 0.0))
    gath[z, y, x, core, rows_dev:pack_rows, :] = packed.astype(BF16)

    if nz & (nz - 1):
        zto = [lax.rem(z + k, nz) for k in range(nz)]
        zof = [lax.rem(z + nz - k, nz) for k in range(nz)]
    else:
        zto = zof = [flip(z, k) for k in range(nz)]
    zpeer = zto[1:]
    xpeer = [lax.rem(x + d, nx) for d in range(1, nx)]
    peers = [(p * 2 + y, tok) for p in zpeer]
    peers += [(z * 2 + oy, tok), (lat, x * 2 + oc)]
    peers += [(lat, p * 2 + core) for p in xpeer]
    barrier = pltpu.get_barrier_semaphore()
    for p in peers:
        pl.semaphore_signal(barrier, inc=1, device_id=p, device_id_type=MESH)
    pl.semaphore_wait(barrier, len(peers))

    sent = []

    def send(src, dst, ssem, rsem, dev):
        cp = pltpu.make_async_remote_copy(src_ref=src, dst_ref=dst, send_sem=ssem,
                                          recv_sem=rsem, device_id=dev, device_id_type=MESH)
        cp.start()
        sent.append(cp)
        return cp

    def move(view, ssem, rsem, dev):
        return send(view, view, ssem, rsem, dev)

    lat_f = lat.astype(F32)
    pair = 2 * rows_dev
    pt = 2 * tpd
    tb = lax.broadcasted_iota(jnp.int32, (pt, pair), 0)
    jb = lax.broadcasted_iota(jnp.int32, (pt, pair), 1)
    diag = jnp.where((jb >= tb * slots) & (jb < (tb + 1) * slots), 1.0, 0.0).astype(BF16)

    def build(zz, yy, xx):
        locs = []
        for c in range(2):
            tags = gath[zz, yy, xx, c, rows_dev:pack_rows, :].astype(F32)
            locs.append(jnp.where(tags[0:1] == lat_f, tags[1:2], -1.0))
        loc = jnp.concatenate(locs, axis=1)
        loc = jnp.broadcast_to(loc, (pt, pair)).astype(BF16)
        rhs = gath[zz, yy, xx, :, 0:rows_dev, :].reshape(pair, block)
        row0 = pl.multiple_of(((zz * 2 + yy) * nx + xx) * pt, pt)
        for b0 in range(0, nb, bstep):
            hot = jnp.concatenate(
                [jnp.where(loc == jnp.asarray(b, BF16), diag, jnp.zeros((), BF16))
                 for b in range(b0, b0 + bstep)], axis=0)
            rows = jnp.dot(hot, rhs, preferred_element_type=F32).astype(BF16)
            for i in range(bstep):
                amat[pl.ds(row0, pt), (b0 + i) * block:(b0 + i + 1) * block] = (
                    rows[i * pt:(i + 1) * pt])

    yp, cp_dev = (z * 2 + oy, tok), (lat, x * 2 + oc)
    xof = [lax.rem(x + nx - 1 - e, nx) for e in range(nx - 1)]
    own.wait()
    zc = [None] + [move(gath.at[z, y, x, core], zs.at[k], zr.at[k], (zto[k] * 2 + y, tok))
                   for k in range(1, nz)]
    xc, vc, dc, cc = {}, {}, {}, {}

    def to_core(k, q, yy, xx):
        v = gath.at[zof[k], yy, xx, core]
        cc[k, q] = move(v, cs.at[k, q], cr.at[k, q], cp_dev)

    for step in range(nz + 3):
        k = step
        if k < nz:
            if k:
                pltpu.make_async_remote_copy(
                    src_ref=gath.at[zof[k], y, x, core], dst_ref=gath.at[zof[k], y, x, core],
                    send_sem=zs.at[k], recv_sem=zr.at[k], device_id=(zto[k] * 2 + y, tok),
                    device_id_type=MESH).wait_recv()
            v = gath.at[zof[k], y, x, core]
            for e in range(nx - 1):
                xc[k, e] = move(v, xs.at[k, e], xr.at[k, e], (lat, xpeer[e] * 2 + core))
            vc[k] = move(v, vs.at[k], vr.at[k], yp)
            to_core(k, 0, y, x)
        stream(4 + 3 * (step + 1))
        k = step - 1
        if 0 <= k < nz:
            for e in range(nx - 1):
                xc[k, e].wait_recv()
                if k % 2 == 0:
                    dc[k, e] = move(gath.at[zof[k], y, xof[e], core], ds.at[k, e], dr.at[k, e], yp)
                to_core(k, 2 + e, y, xof[e])
            vc[k].wait_recv()
            if k % 2:
                for e in range(nx - 1):
                    dc[k, e] = move(gath.at[zof[k], oy, x, core], ds.at[k, e], dr.at[k, e],
                                    (lat, xpeer[e] * 2 + core))
            to_core(k, 1, oy, x)
        k = step - 2
        if 0 <= k < nz:
            for e in range(nx - 1):
                dc[k, e].wait_recv()
                to_core(k, nx + 1 + e, oy, xof[e])
            cc[k, 0].wait_recv()
            build(zof[k], y, x)
            cc[k, 1].wait_recv()
            build(zof[k], oy, x)
            for e in range(nx - 1):
                cc[k, 2 + e].wait_recv()
                build(zof[k], y, xof[e])
        k = step - 3
        if 0 <= k < nz:
            for e in range(nx - 1):
                cc[k, nx + 1 + e].wait_recv()
                build(zof[k], oy, xof[e])
    stream(len(w_copies))

    tokens = amat.shape[0]
    per_lat = tokens // nl

    def matmul(i):
        cols = pl.ds(offs[i], widths[i])

        @pl.loop(0, tokens // mstep)
        def _(m):
            rows = pl.ds(pl.multiple_of(m * mstep, mstep), mstep)
            lats = pl.ds(m * (mstep // (2 * per_lat)), mstep // (2 * per_lat))
            shape = (mstep // (2 * per_lat), 2, per_lat, widths[i])

            def term(k):
                kk = pl.ds(pl.multiple_of(k * kstep, kstep), kstep)
                return jnp.dot(amat[rows, kk], wv[kk, cols],
                               preferred_element_type=F32).reshape(shape)

            part[lats, :, :, cols] = term(0)

            @pl.loop(1, latents // kstep)
            def _(k):
                part[lats, :, :, cols] += term(k)

    def y_start(c):
        cols = pl.ds(c * rw, rw)
        return send(part.at[:, oy, :, cols], yrecv.at[:, :, cols], ys.at[c], yr.at[c], yp)

    def z_start(c, ycp):
        cols = pl.ds(c * rw, rw)
        ycp.wait_recv()
        ysum[:, :, cols] = part[:, y, :, cols] + yrecv[:, :, cols]
        return [send(ysum.at[zto[k], :, cols], zrecv.at[k - 1, :, cols], ps.at[c, k - 1],
                     pr.at[c, k - 1], (zto[k] * 2 + y, tok)) for k in range(1, nz)]

    def finish(c, zcps):
        cols = pl.ds(c * rw, rw)
        total = ysum[z, :, cols] + bias_ref[:, cols]
        for d, cp in enumerate(zcps):
            cp.wait_recv()
            total += zrecv[d, :, cols]
        out_ref[:, cols] = total.astype(out_ref.dtype)

    ycps, zcps = {}, {}
    pend = []
    for i in range(len(widths)):
        for cp in w_copies[w_first[i]:w_first[i + 1]]:
            cp.wait()
        matmul(i)
        now = list(range(offs[i] // rw, (offs[i] + widths[i]) // rw))
        for c in now:
            ycps[c] = y_start(c)
        for c in pend:
            zcps[c] = z_start(c, ycps[c])
        pend = now
    for c in pend:
        zcps[c] = z_start(c, ycps[c])
    for c in zcps:
        finish(c, zcps[c])
    for cp in sent:
        cp.wait_send()


def shards(coefficients, block_ids, counts, decoder, bias):
    nl, nt = lax.axis_size("lat"), lax.axis_size("tok")
    tpd, slots, block = coefficients.shape
    layers, latents, width = decoder.shape
    nb = latents // block
    tokens = tpd * nl * nt
    nz, nx = nl // 2, nt // 2
    per_lat = tokens // nl
    rows_dev = tpd * slots
    pack_rows = rows_dev + 16
    unit = largest_divisor(width, 256, 128)
    widths = [unit]
    while sum(widths) < width:
        widths.append(min(2 * unit, width - sum(widths)))
    rw = 128
    chunks = width // rw
    wsplit = 4
    pieces = sum(wsplit * w // unit for w in widths)
    kstep = largest_divisor(latents, 4096, block)
    mstep = largest_divisor(tokens, 256, 2 * per_lat)
    bstep = largest_divisor(nb, 32, 1)
    cfg = (nl, nt, tpd, slots, block, nb, tuple(widths), rw, kstep, mstep, bstep, wsplit)
    dma = pltpu.SemaphoreType.DMA
    vmem = pl.BlockSpec(memory_space=pltpu.VMEM)
    hbm = pl.BlockSpec(memory_space=pl.ANY)
    flops = 2 * tokens * latents * width
    outs = []
    for layer in range(layers):
        outs.append(pl.pallas_call(
            functools.partial(kernel, cfg),
            out_shape=jax.ShapeDtypeStruct((per_lat, width), BF16),
            in_specs=[pl.BlockSpec(memory_space=pltpu.SMEM), vmem, vmem, hbm, hbm],
            out_specs=vmem,
            scratch_shapes=[
                pltpu.VMEM((nz, 2, nx, 2, pack_rows, block), BF16),
                pltpu.VMEM((latents, width), BF16),
                pltpu.VMEM((tokens, latents), BF16),
                pltpu.VMEM((nz, 2, per_lat, width), F32),
                pltpu.VMEM((nz, per_lat, width), F32),
                pltpu.VMEM((nz, per_lat, width), F32),
                pltpu.VMEM((nz - 1, per_lat, width), F32),
                dma, dma((pieces,)),
                dma((nz,)), dma((nz,)),
                dma((nz, nx - 1)), dma((nz, nx - 1)),
                dma((nz,)), dma((nz,)),
                dma((nz, nx - 1)), dma((nz, nx - 1)),
                dma((nz, 2 * nx)), dma((nz, 2 * nx)),
                dma((chunks,)), dma((chunks,)),
                dma((chunks, nz - 1)), dma((chunks, nz - 1)),
            ],
            compiler_params=pltpu.CompilerParams(
                collective_id=layer, has_side_effects=True, vmem_limit_bytes=66000000),
            cost_estimate=pl.CostEstimate(
                flops=flops, bytes_accessed=latents * width * 2, transcendentals=0),
        )(counts, block_ids, bias[layer:layer + 1], coefficients.reshape(rows_dev, block),
          decoder[layer]))
    return jnp.stack(outs)


def solution(mesh):
    in_specs = (
        P(("lat", "tok"), None, None),
        P(("lat", "tok"), None),
        P(("lat", "tok")),
        P(None, "lat", "tok"),
        P(None, "tok"),
    )
    out_specs = P(None, "lat", "tok")
    return jax.shard_map(shards, mesh=mesh, in_specs=in_specs, out_specs=out_specs, check_vma=False)
```

```python
import functools

import jax
import jax.numpy as jnp
from jax import lax
from jax.experimental import pallas as pl
from jax.experimental.pallas import tpu as pltpu
from jax.sharding import PartitionSpec as P

MESH = pl.DeviceIdType.MESH
F32 = jnp.float32
BF16 = jnp.bfloat16


def largest_divisor(total, limit, unit):
    best = unit
    for size in range(unit, limit + 1, unit):
        if total % size == 0:
            best = size
    return best


def flip(z, k):
    step, out = 1, z
    while step <= k:
        if k & step:
            out = out + step - 2 * step * ((z // step) % 2)
        step *= 2
    return out


def kernel(cfg, counts_ref, ids_ref, bias_ref, coeff_ref, dec_ref, out_ref,
           gath, wv, amat, part, yrecv, ysum, zrecv,
           own_sem, w_sem, zs, zr, xs, xr, vs, vr, ds, dr, cs, cr, ys, yr, ps, pr):
    nl, nt, tpd, slots, block, nb, widths, rw, kstep, mstep, bstep, wsplit = cfg
    nz, nx = nl // 2, nt // 2
    rows_dev = tpd * slots
    pack_rows = gath.shape[4]
    lat, tok = lax.axis_index("lat"), lax.axis_index("tok")
    z, y = lat // 2, lat % 2
    x, core = tok // 2, tok % 2
    oy, oc = 1 - y, 1 - core
    latents = nb * block
    offs = [sum(widths[:i]) for i in range(len(widths))]

    w_copies = []
    for off, w in zip(offs, widths):
        parts = wsplit * w // widths[0]
        for r in range(parts):
            at = (pl.ds(r * (latents // parts), latents // parts), pl.ds(off, w))
            w_copies.append(pltpu.make_async_copy(dec_ref.at[at], wv.at[at],
                                                  w_sem.at[len(w_copies)]))
    w_first = [sum(wsplit * w // widths[0] for w in widths[:i]) for i in range(len(widths) + 1)]
    issued = [0]

    def stream(upto):
        while issued[0] < min(upto, len(w_copies)):
            w_copies[issued[0]].start()
            issued[0] += 1

    own = pltpu.make_async_copy(coeff_ref, gath.at[z, y, x, core, pl.ds(0, rows_dev)], own_sem)
    own.start()
    stream(2)

    ids = ids_ref[...]
    trow = lax.broadcasted_iota(jnp.int32, (tpd, slots), 0)
    scol = lax.broadcasted_iota(jnp.int32, (tpd, slots), 1)
    live_to = jnp.zeros((tpd, slots), jnp.int32)
    for t in range(tpd):
        live_to = jnp.where(trow == t, counts_ref[t], live_to)
    idf = ids.astype(F32)
    owner = jnp.floor((idf + 0.5) * (1.0 / nb))
    within = idf - owner * nb
    owner = jnp.where(scol < live_to, owner, -1.0)
    srow = lax.broadcasted_iota(jnp.int32, (slots, rows_dev), 0)
    jcol = lax.broadcasted_iota(jnp.int32, (slots, rows_dev), 1)
    spread = jnp.where(jcol % slots == srow, 1.0, 0.0).astype(F32)
    t8 = lax.broadcasted_iota(jnp.int32, (tpd, rows_dev), 0)
    j8 = lax.broadcasted_iota(jnp.int32, (tpd, rows_dev), 1)
    mine = (j8 >= t8 * slots) & (j8 < (t8 + 1) * slots)

    def as_row(v):
        wide = jnp.dot(v, spread, preferred_element_type=F32)
        return jnp.sum(jnp.where(mine, wide, 0.0), axis=0, keepdims=True)

    r16 = lax.broadcasted_iota(jnp.int32, (pack_rows - rows_dev, rows_dev), 0)
    packed = jnp.where(r16 == 0, as_row(owner), jnp.where(r16 == 1, as_row(within), 0.0))
    gath[z, y, x, core, rows_dev:pack_rows, :] = packed.astype(BF16)

    if nz & (nz - 1):
        zto = [lax.rem(z + k, nz) for k in range(nz)]
        zof = [lax.rem(z + nz - k, nz) for k in range(nz)]
    else:
        zto = zof = [flip(z, k) for k in range(nz)]
    zpeer = zto[1:]
    xpeer = [lax.rem(x + d, nx) for d in range(1, nx)]
    peers = [(p * 2 + y, tok) for p in zpeer]
    peers += [(z * 2 + oy, tok), (lat, x * 2 + oc)]
    peers += [(lat, p * 2 + core) for p in xpeer]
    barrier = pltpu.get_barrier_semaphore()
    for p in peers:
        pl.semaphore_signal(barrier, inc=1, device_id=p, device_id_type=MESH)
    pl.semaphore_wait(barrier, len(peers))

    sent = []

    def send(src, dst, ssem, rsem, dev):
        cp = pltpu.make_async_remote_copy(src_ref=src, dst_ref=dst, send_sem=ssem,
                                          recv_sem=rsem, device_id=dev, device_id_type=MESH)
        cp.start()
        sent.append(cp)
        return cp

    def move(view, ssem, rsem, dev):
        return send(view, view, ssem, rsem, dev)

    lat_f = lat.astype(F32)
    pair = 2 * rows_dev
    pt = 2 * tpd
    tb = lax.broadcasted_iota(jnp.int32, (pt, pair), 0)
    jb = lax.broadcasted_iota(jnp.int32, (pt, pair), 1)
    diag = jnp.where((jb >= tb * slots) & (jb < (tb + 1) * slots), 1.0, 0.0).astype(BF16)

    def build(zz, yy, xx):
        locs = []
        for c in range(2):
            tags = gath[zz, yy, xx, c, rows_dev:pack_rows, :].astype(F32)
            locs.append(jnp.where(tags[0:1] == lat_f, tags[1:2], -1.0))
        loc = jnp.concatenate(locs, axis=1)
        loc = jnp.broadcast_to(loc, (pt, pair)).astype(BF16)
        rhs = gath[zz, yy, xx, :, 0:rows_dev, :].reshape(pair, block)
        row0 = pl.multiple_of(((zz * 2 + yy) * nx + xx) * pt, pt)
        for b0 in range(0, nb, bstep):
            hot = jnp.concatenate(
                [jnp.where(loc == jnp.asarray(b, BF16), diag, jnp.zeros((), BF16))
                 for b in range(b0, b0 + bstep)], axis=0)
            rows = jnp.dot(hot, rhs, preferred_element_type=F32).astype(BF16)
            for i in range(bstep):
                amat[pl.ds(row0, pt), (b0 + i) * block:(b0 + i + 1) * block] = (
                    rows[i * pt:(i + 1) * pt])

    yp, cp_dev = (z * 2 + oy, tok), (lat, x * 2 + oc)
    xof = [lax.rem(x + nx - 1 - e, nx) for e in range(nx - 1)]
    own.wait()
    zc = [None] + [move(gath.at[z, y, x, core], zs.at[k], zr.at[k], (zto[k] * 2 + y, tok))
                   for k in range(1, nz)]
    xc, vc, dc, cc = {}, {}, {}, {}

    def to_core(k, q, yy, xx):
        v = gath.at[zof[k], yy, xx, core]
        cc[k, q] = move(v, cs.at[k, q], cr.at[k, q], cp_dev)

    for step in range(nz + 3):
        k = step
        if k < nz:
            if k:
                pltpu.make_async_remote_copy(
                    src_ref=gath.at[zof[k], y, x, core], dst_ref=gath.at[zof[k], y, x, core],
                    send_sem=zs.at[k], recv_sem=zr.at[k], device_id=(zto[k] * 2 + y, tok),
                    device_id_type=MESH).wait_recv()
            v = gath.at[zof[k], y, x, core]
            for e in range(nx - 1):
                xc[k, e] = move(v, xs.at[k, e], xr.at[k, e], (lat, xpeer[e] * 2 + core))
            vc[k] = move(v, vs.at[k], vr.at[k], yp)
            to_core(k, 0, y, x)
        stream(4 + 3 * (step + 1))
        k = step - 1
        if 0 <= k < nz:
            for e in range(nx - 1):
                xc[k, e].wait_recv()
                if k % 2 == 0:
                    dc[k, e] = move(gath.at[zof[k], y, xof[e], core], ds.at[k, e], dr.at[k, e], yp)
                to_core(k, 2 + e, y, xof[e])
            vc[k].wait_recv()
            if k % 2:
                for e in range(nx - 1):
                    dc[k, e] = move(gath.at[zof[k], oy, x, core], ds.at[k, e], dr.at[k, e],
                                    (lat, xpeer[e] * 2 + core))
            to_core(k, 1, oy, x)
        k = step - 2
        if 0 <= k < nz:
            for e in range(nx - 1):
                dc[k, e].wait_recv()
                to_core(k, nx + 1 + e, oy, xof[e])
            cc[k, 0].wait_recv()
            build(zof[k], y, x)
            cc[k, 1].wait_recv()
            build(zof[k], oy, x)
            for e in range(nx - 1):
                cc[k, 2 + e].wait_recv()
                build(zof[k], y, xof[e])
        k = step - 3
        if 0 <= k < nz:
            for e in range(nx - 1):
                cc[k, nx + 1 + e].wait_recv()
                build(zof[k], oy, xof[e])
    stream(len(w_copies))

    tokens = amat.shape[0]
    per_lat = tokens // nl

    def matmul(i, between):
        cols = pl.ds(offs[i], widths[i])
        ksteps = latents // kstep
        for k in range(ksteps):
            kk = pl.ds(k * kstep, kstep)

            @pl.loop(0, tokens // mstep)
            def _(m):
                rows = pl.ds(pl.multiple_of(m * mstep, mstep), mstep)
                lats = pl.ds(m * (mstep // (2 * per_lat)), mstep // (2 * per_lat))
                shape = (mstep // (2 * per_lat), 2, per_lat, widths[i])
                term = jnp.dot(amat[rows, kk], wv[kk, cols],
                               preferred_element_type=F32).reshape(shape)
                if k == 0:
                    part[lats, :, :, cols] = term
                else:
                    part[lats, :, :, cols] += term

            if k == ksteps * 3 // 4 - 1:
                between()

    def y_start(c):
        cols = pl.ds(c * rw, rw)
        return send(part.at[:, oy, :, cols], yrecv.at[:, :, cols], ys.at[c], yr.at[c], yp)

    def z_start(c, ycp):
        cols = pl.ds(c * rw, rw)
        ycp.wait_recv()
        ysum[:, :, cols] = part[:, y, :, cols] + yrecv[:, :, cols]
        return [send(ysum.at[zto[k], :, cols], zrecv.at[k - 1, :, cols], ps.at[c, k - 1],
                     pr.at[c, k - 1], (zto[k] * 2 + y, tok)) for k in range(1, nz)]

    def finish(c, zcps):
        cols = pl.ds(c * rw, rw)
        total = ysum[z, :, cols] + bias_ref[:, cols]
        for d, cp in enumerate(zcps):
            cp.wait_recv()
            total += zrecv[d, :, cols]
        out_ref[:, cols] = total.astype(out_ref.dtype)

    ycps, zcps = {}, {}
    pend = []
    for i in range(len(widths)):
        for cp in w_copies[w_first[i]:w_first[i + 1]]:
            cp.wait()

        def early():
            if pend:
                zcps[pend[0]] = z_start(pend[0], ycps[pend[0]])

        matmul(i, early)
        now = list(range(offs[i] // rw, (offs[i] + widths[i]) // rw))
        for c in now:
            ycps[c] = y_start(c)
        for c in pend:
            if c not in zcps:
                zcps[c] = z_start(c, ycps[c])
        pend = now
    for c in pend:
        zcps[c] = z_start(c, ycps[c])
    for c in zcps:
        finish(c, zcps[c])
    for cp in sent:
        cp.wait_send()


def shards(coefficients, block_ids, counts, decoder, bias):
    nl, nt = lax.axis_size("lat"), lax.axis_size("tok")
    tpd, slots, block = coefficients.shape
    layers, latents, width = decoder.shape
    nb = latents // block
    tokens = tpd * nl * nt
    nz, nx = nl // 2, nt // 2
    per_lat = tokens // nl
    rows_dev = tpd * slots
    pack_rows = rows_dev + 16
    unit = largest_divisor(width, 640, 128)
    widths = [unit]
    while sum(widths) < width:
        widths.append(unit)
    rw = 128
    chunks = width // rw
    wsplit = 8
    pieces = sum(wsplit * w // unit for w in widths)
    kstep = largest_divisor(latents, 2048, block)
    mstep = largest_divisor(tokens, 256, 2 * per_lat)
    bstep = largest_divisor(nb, 32, 1)
    cfg = (nl, nt, tpd, slots, block, nb, tuple(widths), rw, kstep, mstep, bstep, wsplit)
    dma = pltpu.SemaphoreType.DMA
    vmem = pl.BlockSpec(memory_space=pltpu.VMEM)
    hbm = pl.BlockSpec(memory_space=pl.ANY)
    flops = 2 * tokens * latents * width
    outs = []
    for layer in range(layers):
        outs.append(pl.pallas_call(
            functools.partial(kernel, cfg),
            out_shape=jax.ShapeDtypeStruct((per_lat, width), BF16),
            in_specs=[pl.BlockSpec(memory_space=pltpu.SMEM), vmem, vmem, hbm, hbm],
            out_specs=vmem,
            scratch_shapes=[
                pltpu.VMEM((nz, 2, nx, 2, pack_rows, block), BF16),
                pltpu.VMEM((latents, width), BF16),
                pltpu.VMEM((tokens, latents), BF16),
                pltpu.VMEM((nz, 2, per_lat, width), F32),
                pltpu.VMEM((nz, per_lat, width), F32),
                pltpu.VMEM((nz, per_lat, width), F32),
                pltpu.VMEM((nz - 1, per_lat, width), F32),
                dma, dma((pieces,)),
                dma((nz,)), dma((nz,)),
                dma((nz, nx - 1)), dma((nz, nx - 1)),
                dma((nz,)), dma((nz,)),
                dma((nz, nx - 1)), dma((nz, nx - 1)),
                dma((nz, 2 * nx)), dma((nz, 2 * nx)),
                dma((chunks,)), dma((chunks,)),
                dma((chunks, nz - 1)), dma((chunks, nz - 1)),
            ],
            compiler_params=pltpu.CompilerParams(
                collective_id=layer, has_side_effects=True, vmem_limit_bytes=66000000),
            cost_estimate=pl.CostEstimate(
                flops=flops, bytes_accessed=latents * width * 2, transcendentals=0),
        )(counts, block_ids, bias[layer:layer + 1], coefficients.reshape(rows_dev, block),
          decoder[layer]))
    return jnp.stack(outs)


def solution(mesh):
    in_specs = (
        P(("lat", "tok"), None, None),
        P(("lat", "tok"), None),
        P(("lat", "tok")),
        P(None, "lat", "tok"),
        P(None, "tok"),
    )
    out_specs = P(None, "lat", "tok")
    return jax.shard_map(shards, mesh=mesh, in_specs=in_specs, out_specs=out_specs, check_vma=False)
```
